32 devices in a mesh: aux: 8 (over y, x, core), shell: 4 (over z).
Axes of the slice: x: 2, y: 2, z: 4, core: 2. Of those that a mesh axis runs over, the one named last changes fastest.
Arguments:
- density: bfloat16 [32, 120, 8192], P('aux', None, 'shell'), may hold values from -6 to 6
- occ_density: bfloat16 [32, 120, 120], P('aux'), may hold values from -6 to 6
- cabs_coeff: bfloat16 [2048, 8192], P('aux', 'shell'), may hold values from -0.0625 to 0.0625
- occ_coeff: bfloat16 [2048, 120], P('aux'), may hold values from -0.5 to 0.5
- tile_owner: int32 [16, 1], replicated, may hold values from 0 to 3; in each aligned block of 16 rows (0 to 15, 16 to 31, ...) at most 8 rows name the same one
Outputs:
- ao_density: bfloat16 [32, 32, 128, 2048], P('shell', 'aux')
The draws below stay inside these ranges and needn't reach their ends.
Inputs may be any that keep to these rules, and one draw needn't show every extreme that they name: `tile_owner`: no owner holds more than 8 blocks, and some owner holds exactly 8; every owner holds at least one block.
All inputs are finite; a program needn't handle non-finite values.
Results may differ from the reference program's by a relative error of at most 0.015.
Values may be sent and summed in bfloat16 or wider, within the bound.
No kernel may reach another device: no remote copies, remote signals or barrier semaphores. Data moves between devices by JAX's collectives and lax.ppermute only.
A program may use at most 64 MiB of HBM per device.

```python
import math
import jax
import jax.numpy as jnp
import numpy as np
from jax import lax

NOCC = 120
NAO = 2048
NCABS = 8192
CAPT = 8
NTILE = 16
BW = 128
NAUX = 32
N_SHELL = 4


def level_of(rng, extent, shards, low, high):
    loudness = 1.0
    for dim, parts in shards:
        draws = jax.random.uniform(jax.random.fold_in(jax.random.fold_in(rng, 6), dim), (parts,), jnp.float32, low / len(shards), high / len(shards))
        loudness = loudness * jnp.repeat(jnp.exp(draws), extent[dim] // parts).reshape((-1,) + (1,) * (len(extent) - 1 - dim))
    return loudness


def shared_out(own_key, own, number, rows, number_of, top, limit, skew):
    ranking = jax.random.permutation(own_key, number_of)
    packed, common = portions_of(number_of, rows * top, limit, skew, True), portions_of(number_of, rows * top, limit, skew, False)
    places = jnp.arange(number_of)

    def named(tallies, offset_by):
        used = int((tallies > 0).sum())
        fixed = max(1, used // 4)
        passed = fixed + (places - fixed + offset_by * (used - fixed)) % max(1, number_of - fixed)
        return jnp.zeros((number_of,), jnp.int32).at[ranking[jnp.where(places < fixed, places, passed)]].set(jnp.asarray(tallies, jnp.int32))

    tallies = jnp.where(number % 4 == 0, named(packed, number // 4), named(common, number - number // 4 - 1))
    mixed = jax.random.permutation(jax.random.fold_in(own, 3), number_of)
    giver, taker = mixed[0:number_of // 2 * 2:2], mixed[1:number_of // 2 * 2:2]
    slack = jnp.minimum(tallies[giver] - 1, limit - tallies[taker]) // 2
    slack = jnp.where((giver == ranking[0]) | (taker == ranking[0]) | (tallies[taker] == 0), 0, jnp.maximum(slack, 0))
    passed = jax.random.randint(jax.random.fold_in(own, 4), (number_of // 2,), 0, 1 << 20) % (slack + 1)
    tallies = tallies.at[giver].add(-passed).at[taker].add(passed)
    members = jnp.searchsorted(jnp.cumsum(tallies), jnp.arange(rows * top), side="right").astype(jnp.int32)
    grid = members.reshape(top, rows).T
    grid = grid[jax.random.permutation(jax.random.fold_in(own, 1), rows)]
    offset_by = jax.random.randint(jax.random.fold_in(own, 2), (rows, 1), 0, top)
    return jnp.take_along_axis(grid, (jnp.arange(top)[None, :] + offset_by) % top, axis=1)


def portions_of(number_of, total, limit, skew, full):
    weights = [(1 << 20) // math.isqrt(grade ** skew) + 1 for grade in range(1, number_of + 1)]
    largest = limit if full else min(limit, max(-(-total // number_of), total * weights[0] // sum(weights)))
    least = 1 if total - largest >= number_of - 1 else 0
    counts, spare = [largest] + [least] * (number_of - 1), total - largest - least * (number_of - 1)
    while spare > 0:
        candidates = [i for i in range(1, number_of) if counts[i] < largest] or [i for i in range(1, number_of) if counts[i] < limit]
        whole, left = sum([weights[i] for i in candidates]), spare
        for i in candidates:
            more = min(limit - counts[i], max(1, left * weights[i] // whole), spare)
            counts[i] = counts[i] + more
            spare = spare - more
    return np.array(counts)


def gaussian(rng, shape, scale, reach, cuts=(), kind=jnp.bfloat16):
    drawn = scale * jax.random.normal(rng, shape, jnp.float32)
    if cuts:
        drawn = drawn * level_of(rng, shape, cuts, -0.22, 0.18)
    return jnp.clip(drawn, -reach, reach).astype(kind)


def setup_inputs(seed: int = 0) -> dict:
    splits = jax.random.split(jax.random.key(seed), 6)
    density = gaussian(splits[0], (NAUX, NOCC, NCABS), 1.0, 6.0, ((0, 8), (2, 4)))
    occ_density = gaussian(splits[1], (NAUX, NOCC, NOCC), 1.0, 6.0, ((0, 8),))
    cabs_coeff = gaussian(splits[2], (NAO, NCABS), NCABS ** -0.5, 0.0625, ((0, 8), (1, 4)))
    occ_coeff = gaussian(splits[3], (NAO, NOCC), NOCC ** -0.5, 0.5, ((0, 8),))
    tile_owner_keys = jax.random.split(jax.random.fold_in(splits[4], 1), NTILE // NTILE)
    tile_owner_turns = jax.random.permutation(jax.random.fold_in(splits[4], 3), NTILE // NTILE)
    tile_owner = jax.vmap(lambda own, number: shared_out(jax.random.fold_in(splits[4], 2), own, number, NTILE, N_SHELL, 1, CAPT, 2))(tile_owner_keys, tile_owner_turns).reshape((NTILE, 1))
    return {"density": density, "occ_density": occ_density, "cabs_coeff": cabs_coeff, "occ_coeff": occ_coeff, "tile_owner": tile_owner}


def reference(density, occ_density, cabs_coeff, occ_coeff, tile_owner):
    count = density.shape[0]
    flat = density.reshape(count * NOCC, NCABS)
    cshard = NCABS // N_SHELL

    def add_shard(total, shard):
        start = (shard * cshard).astype(jnp.int32)
        rows = lax.dynamic_slice_in_dim(flat, start, cshard, 1)
        cols = lax.dynamic_slice_in_dim(cabs_coeff, start, cshard, 1)
        part = lax.dot_general(rows, cols, (((1,), (1,)), ((), ())), preferred_element_type=jnp.float32)
        part = lax.optimization_barrier(part.astype(jnp.bfloat16))
        return total + part.astype(jnp.float32), None

    cabs, unused = lax.scan(add_shard, jnp.zeros((count * NOCC, NAO), jnp.float32), jnp.arange(N_SHELL, dtype=jnp.int32))
    occ_term = jnp.einsum("qij,nj->qin", occ_density.astype(jnp.float32), occ_coeff.astype(jnp.float32), precision=lax.Precision.HIGHEST)
    half = (cabs.reshape(count, NOCC, NAO) + occ_term).astype(jnp.bfloat16)
    blocks = half.astype(jnp.float32).reshape(count, NOCC, NTILE, BW)
    owners = tile_owner[:, 0]
    coeff = occ_coeff.astype(jnp.float32)

    def one_owner(owner):
        owned = (owners == owner).astype(jnp.int32)
        rank = jnp.cumsum(owned) - 1
        select = ((rank[None, :] == jnp.arange(CAPT, dtype=jnp.int32)[:, None]) & (owned[None, :] == 1)).astype(jnp.float32)
        picked = jnp.einsum("kt,qitw->kqiw", select, blocks, precision=lax.Precision.HIGHEST)
        result = jnp.einsum("kqiw,mi->kqwm", picked, coeff, precision=lax.Precision.HIGHEST)
        return result.astype(jnp.bfloat16)

    stacked = lax.map(one_owner, jnp.arange(N_SHELL, dtype=jnp.int32))
    return stacked.reshape(N_SHELL * CAPT, count, BW, NAO)
```

```python
import functools
import math

import jax
import jax.numpy as jnp
from jax import lax
from jax.experimental import pallas as pl
from jax.experimental.pallas import tpu as pltpu
from jax.sharding import PartitionSpec as P

CAPT = 8
LANES = 128
CORES = 2
GRANT = 12 * 1024 * 1024
VMEM = pl.BlockSpec(memory_space=pltpu.VMEM)
ANY = pl.BlockSpec(memory_space=pl.ANY)
SMEM = pl.BlockSpec(memory_space=pltpu.SMEM)


def call(kernel, out_shape, in_specs, out_specs, flops, size, scratch=(), aliases=None):
    return pl.pallas_call(
        kernel,
        out_shape=out_shape,
        in_specs=in_specs,
        out_specs=out_specs,
        scratch_shapes=list(scratch),
        input_output_aliases=aliases or {},
        compiler_params=pltpu.CompilerParams(vmem_limit_bytes=GRANT),
        cost_estimate=pl.CostEstimate(flops=flops, bytes_accessed=size, transcendentals=0),
    )


def matmul_kernel(left_ref, occ_ref, first_ref, second_ref, out_ref):
    depth, nocc = left_ref.shape[1], occ_ref.shape[1]
    rows = first_ref.shape[0]
    dims = (((1,), (1,)), ((), ()))
    for k, right_ref in enumerate((first_ref, second_ref)):
        cols = slice(k * rows, (k + 1) * rows)

        def product():
            return lax.dot_general(
                left_ref[...], right_ref[:, :depth], dims, preferred_element_type=jnp.float32
            )

        @pl.when(lax.axis_index("shell") == 0)
        def _():
            occ = lax.dot_general(
                occ_ref[...],
                right_ref[:, depth : depth + nocc],
                dims,
                preferred_element_type=jnp.float32,
            )
            out_ref[:, cols] = (product() + occ).astype(out_ref.dtype)

        @pl.when(lax.axis_index("shell") != 0)
        def _():
            out_ref[:, cols] = product().astype(out_ref.dtype)


def matmul(left, occ, first, second):
    rows, depth = left.shape
    cols = 2 * first.shape[0]
    return call(
        matmul_kernel,
        jax.ShapeDtypeStruct((rows, cols), left.dtype),
        [VMEM] * 4,
        VMEM,
        2 * rows * depth * cols,
        2 * (rows + cols) * depth,
    )(left, occ, first, second)


def send_kernel(owners, groups, *refs):
    me = lax.axis_index("shell")
    outs = refs[-len(groups) :]
    at = 0
    for out_ref, hops in zip(outs, groups):
        for hop in hops:
            part_ref = refs[at]
            before_ref = refs[at + 1] if hop else None
            at += 2 if hop else 1

            def write(part_ref=part_ref, before_ref=before_ref, out_ref=out_ref):
                if before_ref is None:
                    out_ref[...] = part_ref[...]
                else:
                    out_ref[...] = part_ref[...] + before_ref[...]

            pl.when((me == hop) | (me == owners - 1 - hop))(write)


def send(owners, groups, values):
    flat = [v for hops in values for pair in hops for v in pair]
    shape = jax.ShapeDtypeStruct(flat[0].shape, flat[0].dtype)
    size = 2 * math.prod(shape.shape)
    return call(
        functools.partial(send_kernel, owners, groups),
        [shape] * len(groups),
        [VMEM] * len(flat),
        [VMEM] * len(groups),
        size * len(groups),
        3 * size * len(groups),
    )(*flat)


def zero_kernel(owner_ref, out_ref, zero, sem):
    me = lax.axis_index("shell")
    count = jnp.int32(0)
    for tile in range(owner_ref.shape[0]):
        count += jnp.where(owner_ref[tile] == me, 1, 0)
    zero[...] = jnp.zeros_like(zero)
    for wait in (False, True):
        for slot in range(out_ref.shape[0]):

            @pl.when(slot >= count)
            def _():
                for q in range(out_ref.shape[1]):
                    copy = pltpu.make_async_copy(zero, out_ref.at[slot, q], sem.at[slot, q])
                    copy.wait() if wait else copy.start()


def zero_slots(owner, shape, dtype):
    return call(
        zero_kernel,
        jax.ShapeDtypeStruct(shape, dtype),
        [SMEM],
        ANY,
        0,
        math.prod(shape),
        [pltpu.VMEM(shape[2:], dtype), pltpu.SemaphoreType.DMA(shape[:2])],
    )(owner)


def occ_kernel(number, depth, table_ref, first_ref, second_ref, *refs):
    out_ref, sem = refs[-2:]
    me = lax.axis_index("aux")
    rows = first_ref.shape[0]
    copies = []
    for k, piece in enumerate((first_ref, second_ref)):
        start = pl.multiple_of(table_ref[number, me ^ k] * rows, 8)
        copies.append(
            pltpu.make_async_copy(
                piece.at[:, pl.ds(depth, LANES)], out_ref.at[pl.ds(start, rows)], sem.at[k]
            )
        )
    for copy in copies:
        copy.start()
    for copy in copies:
        copy.wait()


def put_occ(table, number, first, second, nao, depth, before):
    rows = first.shape[0]
    old = [] if before is None else [before]
    return call(
        functools.partial(occ_kernel, number, depth),
        jax.ShapeDtypeStruct((nao, LANES), first.dtype),
        [SMEM] + [ANY] * (2 + len(old)),
        ANY,
        0,
        8 * rows * LANES,
        [pltpu.SemaphoreType.DMA((2,))],
        {3: 0} if old else None,
    )(table, first, second, *old)


def final_kernel(nocc, chunk, near_of, owner_ref, table_ref, *refs):
    parts, occ_ref, out_ref, stage, sem = refs[: len(near_of)], *refs[-5:-4], *refs[-3:]
    me, here = lax.axis_index("aux"), lax.axis_index("shell")
    span, width = out_ref.shape[1], out_ref.shape[2]
    tiles = parts[0].shape[1] // width
    ntile = owner_ref.shape[0]
    for t in range(tiles):
        source = table_ref[chunk, me ^ (t * 2 // tiles)]
        tile = source * (tiles // 2) + t % (tiles // 2)
        slot = jnp.int32(0)
        for other in range(ntile):
            slot += jnp.where((owner_ref[other] == here) & (other < tile), 1, 0)

        @pl.when(owner_ref[tile] == here)
        def _(t=t, slot=slot):
            copies = []
            for q in range(span):
                rows, cols = pl.ds(q * nocc, nocc), pl.ds(t * width, width)
                half = jnp.zeros((nocc, width), jnp.float32)
                for part, hops in zip(parts, near_of):
                    value = part[rows, cols].astype(jnp.float32)
                    if hops is not None:
                        near = functools.reduce(
                            jnp.logical_or, [(here == h) for h in hops]
                        )
                        value = jnp.where(near, value, 0.0)
                    half = half + value
                half = half.astype(out_ref.dtype)
                stage[q] = lax.dot_general(
                    half,
                    occ_ref[:, pl.ds(0, nocc)],
                    (((0,), (1,)), ((), ())),
                    preferred_element_type=jnp.float32,
                ).astype(out_ref.dtype)
                copy = pltpu.make_async_copy(stage.at[q], out_ref.at[slot, q], sem.at[q])
                copy.start()
                copies.append(copy)
            for copy in copies:
                copy.wait()


def final(owner, table, chunk, parts, near_of, occ_full, out, nocc):
    _, span, width, nao = out.shape
    tiles = parts[0].shape[1] // width
    return call(
        functools.partial(final_kernel, nocc, chunk, near_of),
        jax.ShapeDtypeStruct(out.shape, out.dtype),
        [SMEM, SMEM] + [VMEM] * (len(parts) + 1) + [ANY],
        ANY,
        span * nocc * width * nao * tiles,
        span * width * nao * tiles,
        [pltpu.VMEM((span, width, nao), out.dtype), pltpu.SemaphoreType.DMA((span,))],
        {len(parts) + 3: 0},
    )(owner, table, *parts, occ_full, out)


def side_of(chips):
    side = math.isqrt(chips)
    while chips % side:
        side -= 1
    return side


def gather_rounds(aux):
    chips = aux // CORES
    nx = side_of(chips)
    ny = chips // nx

    def chip(y, x):
        return (y % ny) * nx + x % nx

    rounds = [(list(range(aux)), None, None)]
    index = {(0, 0): 0}
    order = [(a, 0) for a in range(1, nx)] + [(0, b) for b in range(1, ny)]
    order += [(a, b) for a in range(1, nx) for b in range(1, ny)]
    for a, b in order:
        source, pairs = [], []
        for d in range(aux):
            c, (y, x) = d % CORES, divmod(d // CORES, nx)
            turn = nx == ny and c == 1
            dx, dy = (b, a) if turn else (a, b)
            source.append(chip(y + dy, x + dx) * CORES + c)
            if a and b:
                dx, dy = (0, a) if turn else (a, 0)
            pairs.append((chip(y + dy, x + dx) * CORES + c, d))
        index[a, b] = len(rounds)
        rounds.append((source, pairs, index[0, b] if a and b else 0))
    return rounds


def per_device(density, occ_density, cabs_coeff, occ_coeff, tile_owner):
    local_q, nocc, depth = density.shape
    aux, owners = lax.axis_size("aux"), lax.axis_size("shell")
    rows = cabs_coeff.shape[0]
    nao = rows * aux
    ntile = tile_owner.shape[0]
    width = nao // ntile

    lanes = ((0, 0), (0, LANES - nocc))
    mine = jnp.concatenate([cabs_coeff, jnp.pad(occ_coeff, lanes)], axis=1)
    left = density.reshape(local_q * nocc, depth)
    occ = occ_density.reshape(local_q * nocc, nocc)
    owner = tile_owner.reshape(ntile)

    rounds = gather_rounds(aux)
    count = len(rounds)
    table = jnp.asarray([source for source, _, _ in rounds], jnp.int32)
    swap = [(d, d ^ 1) for d in range(aux)]
    hops = owners - 1
    half = (hops + 1) // 2
    arrived, pieces, partial, got = [], [], {}, {}

    def arrive(number):
        _, pairs, origin = rounds[number]
        value = mine
        if pairs is not None:
            value = arrived[origin]
            if number > 1:
                value = lax.optimization_barrier((value, arrived[-1]))[0]
            value = lax.ppermute(value, "aux", pairs)
        arrived.append(value)
        other = lax.ppermute(value, "aux", swap)
        pieces.append((value, other))
        partial[number] = matmul(left, occ, value, other)

    def terms(chunk):
        parts, near_of = [partial[chunk]], [None]
        for hop in range(hops):
            parts.append(got[chunk, hop])
            near_of.append(sorted({hop + 1, owners - 2 - hop}))
        return parts, near_of

    out = zero_slots(owner, (CAPT, local_q, width, nao), density.dtype)
    arrive(0)
    occ_full = None
    for step in range(count + hops):
        groups, values = [], []
        for hop in range(half):
            shared = [
                h for h in sorted({hop, hops - 1 - hop}) if 0 <= step - h < count
            ]
            if shared:
                groups.append(shared)
                values.append(
                    [
                        (partial[step - h],) + ((got[step - h, h - 1],) if h else ())
                        for h in shared
                    ]
                )
        new = {}
        if groups:
            if groups == [[0]]:
                sent = [values[0][0][0]]
            else:
                sent = send(owners, groups, values)
            for shared, value in zip(groups, sent):
                pairs = []
                for h in shared:
                    pairs += [(h, h + 1), (owners - 1 - h, owners - 2 - h)]
                result = lax.ppermute(value, "shell", pairs)
                for h in shared:
                    new[step - h, h] = result
        if step < count:
            first, second = pieces[step]
            occ_full = put_occ(table, step, first, second, nao, depth, occ_full)
        if step + 1 < count:
            arrive(step + 1)
        if step >= hops:
            chunk = step - hops
            parts, near_of = terms(chunk)
            out = final(owner, table, chunk, parts, near_of, occ_full, out, nocc)
        got.update(new)
    return out


def solution(mesh):
    in_specs = (
        P("aux", None, "shell"),
        P("aux", None, None),
        P("aux", "shell"),
        P("aux", None),
        P(),
    )
    out_specs = P("shell", "aux", None, None)

    return jax.shard_map(
        per_device, mesh=mesh, in_specs=in_specs, out_specs=out_specs, check_vma=False
    )
```
